32 devices in a mesh: slab: 32 (over z, y, x, core).
Axes of the slice: x: 2, y: 2, z: 4, core: 2. Of those that a mesh axis runs over, the one named last changes fastest.
Arguments:
- offsets: float32 [2, 32, 16, 128], P(None, 'slab'), may hold values from 0 to 1
- velocity: float32 [2, 32, 16, 128], P(None, 'slab'), may hold values from -4 to 4
- affine: float32 [4, 32, 16, 128], P(None, 'slab'), may hold values from -1.5 to 1.5
- strain: float32 [4, 32, 16, 128], P(None, 'slab'), may hold values from -0.3 to 0.3
- tile_fill: int32 [32, 16], P('slab'), may hold values from 32 to 128
- force_field: float32 [2, 128, 1024], P(None, 'slab'), may hold values from -6 to 6
- cotangent: float32 [12, 32, 16, 128], P(None, 'slab'), may hold values from -6 to 6
Outputs:
- state_grad: float32 [12, 32, 16, 128], P(None, 'slab')
- force_grad: float32 [2, 128, 1024], P(None, 'slab')
The draws below stay inside these ranges and needn't reach their ends.
All inputs are finite; a program needn't handle non-finite values.
Results may differ from the reference program's by a relative error of at most 0.0003.
Values sent between devices are 32-bit elements; how exact they have to be, the bound alone decides.
A program may use at most 64 MiB of HBM per device.

```python
from functools import partial
import jax
import jax.numpy as jnp
from jax import lax

BR = 4
BC = 64
P_SIZE = 128
STEPS = 4
NCB = 16
BANDS = 32
ROWS = 128
W = 1024


def place_ends(values, stream_key, smallest, high):
    index_at = [jax.random.randint(jax.random.fold_in(stream_key, axis), (), 0, length) for axis, length in enumerate(values.shape)]
    longest = values.shape.index(max(values.shape))
    beside = index_at[:longest] + [(index_at[longest] + 1) % values.shape[longest]] + index_at[longest + 1:]
    return values.at[tuple(index_at)].set(smallest).at[tuple(beside)].set(high)


def shard_levels(stream_key, dims, split, least, high):
    gain = 1.0
    for axis_at, shards_of in split:
        draws = jax.random.uniform(jax.random.fold_in(jax.random.fold_in(stream_key, 6), axis_at), (shards_of,), jnp.float32, least / len(split), high / len(split))
        gain = gain * jnp.repeat(jnp.exp(draws), dims[axis_at] // shards_of).reshape((-1,) + (1,) * (len(dims) - 1 - axis_at))
    return gain


def bell_draw(own_key, shape, width, limit, split=(), held_as=jnp.bfloat16):
    values = width * jax.random.normal(own_key, shape, jnp.float32)
    if split:
        values = values * shard_levels(own_key, shape, split, -0.22, 0.18)
    return jnp.clip(values, -limit, limit).astype(held_as)


def setup_inputs(seed: int = 0) -> dict:
    splits = jax.random.split(jax.random.key(seed), 8)
    offsets = jnp.clip(1.0 * jax.random.uniform(splits[0], (2, BANDS, NCB, P_SIZE), jnp.float32) ** shard_levels(splits[0], (2, BANDS, NCB, P_SIZE), ((1, 32),), -0.2, 0.2), 0.0, 1.0)
    velocity = bell_draw(splits[1], (2, BANDS, NCB, P_SIZE), 1.0, 4.0, ((1, 32),), jnp.float32)
    affine = bell_draw(splits[2], (4, BANDS, NCB, P_SIZE), 0.3, 1.5, ((1, 32),), jnp.float32)
    strain = bell_draw(splits[3], (4, BANDS, NCB, P_SIZE), 0.08, 0.3, ((1, 32),), jnp.float32)
    tile_fill = place_ends(jax.random.randint(splits[4], (BANDS, NCB), P_SIZE // 4, P_SIZE + 1), jax.random.fold_in(splits[4], 1), P_SIZE // 4, P_SIZE).astype(jnp.int32)
    force_field = bell_draw(splits[5], (2, ROWS, W), 1.0, 6.0, ((1, 32),), jnp.float32)
    cotangent = bell_draw(splits[6], (12, BANDS, NCB, P_SIZE), 1.0, 6.0, ((1, 32),), jnp.float32)
    return {"offsets": offsets, "velocity": velocity, "affine": affine, "strain": strain, "tile_fill": tile_fill, "force_field": force_field, "cotangent": cotangent}


time_step = 0.1
shear_modulus = 2.0
bulk_modulus = 2.0
particle_mass = 1.0
mass_floor = 0.25
stress_factor = -0.4
highest = lax.Precision.HIGHEST

def spline(distance):
    magnitude = jnp.abs(distance)
    inside = 0.75 - magnitude * magnitude
    outside = 0.5 * jnp.square(jnp.maximum(1.5 - magnitude, 0.0))
    return jnp.where(magnitude < 0.5, inside, outside)

def band_weights(position):
    row_nodes = jnp.arange(2 * BR, dtype=jnp.float32)
    col_nodes = jnp.arange(2 * BC, dtype=jnp.float32)
    row_dist = row_nodes[None, None, :] - position[0][:, :, None]
    col_dist = col_nodes[None, None, :] - position[1][:, :, None]
    return (spline(row_dist), spline(col_dist), row_dist, col_dist)

def scatter_band(particles, alive_mask):
    row_weight, col_weight, row_dist, col_dist = band_weights(particles[0:2])
    upper_left, upper_right = (particles[8], particles[9])
    lower_left, lower_right = (particles[10], particles[11])
    jacobian = upper_left * lower_right - upper_right * lower_left
    pressure = bulk_modulus * (jacobian - 1.0) * jacobian
    stress_xx = shear_modulus * (upper_left * upper_left + upper_right * upper_right - 1.0) + pressure
    stress_xy = shear_modulus * (upper_left * lower_left + upper_right * lower_right)
    stress_yy = shear_modulus * (lower_left * lower_left + lower_right * lower_right - 1.0) + pressure
    masses = particle_mass * alive_mask
    moment_xx = alive_mask * stress_factor * stress_xx + masses * particles[4]
    moment_xy = alive_mask * stress_factor * stress_xy + masses * particles[5]
    moment_yx = alive_mask * stress_factor * stress_xy + masses * particles[6]
    moment_yy = alive_mask * stress_factor * stress_yy + masses * particles[7]
    plain_part = jnp.stack([row_weight * masses[:, :, None], row_weight * (masses * particles[2])[:, :, None] + row_weight * row_dist * moment_xx[:, :, None], row_weight * (masses * particles[3])[:, :, None] + row_weight * row_dist * moment_yx[:, :, None]], axis=2)
    slope_part = jnp.stack([jnp.zeros_like(row_weight), row_weight * moment_xy[:, :, None], row_weight * moment_yy[:, :, None]], axis=2)
    window_sum = jnp.einsum('cpkr,cpj->krcj', plain_part, col_weight, precision=highest)
    window_sum = window_sum + jnp.einsum('cpkr,cpj->krcj', slope_part, col_weight * col_dist, precision=highest)
    col_slots = window_sum[..., :BC] + jnp.roll(window_sum[..., BC:], 1, axis=2)
    blocks = col_slots.shape[2]
    return jnp.roll(col_slots.reshape(3, 2 * BR, blocks * BC), -(BC // 2), axis=-1)

def gather_band(particles, band_velocity):
    position = particles[0:2]
    row_weight, col_weight, row_dist, col_dist = band_weights(position)
    blocks = particles.shape[1]
    shifted = jnp.roll(band_velocity, BC // 2, axis=-1).reshape(2, 2 * BR, blocks, BC)
    windows = jnp.concatenate([shifted, jnp.roll(shifted, -1, axis=2)], axis=-1)
    plain_part = jnp.einsum('cpj,arcj->acpr', col_weight, windows, precision=highest)
    slope_part = jnp.einsum('cpj,arcj->acpr', col_weight * col_dist, windows, precision=highest)
    new_velocity = lax.optimization_barrier(jnp.sum(row_weight[None] * plain_part, axis=-1))
    along_rows = 4.0 * lax.optimization_barrier(jnp.sum((row_weight * row_dist)[None] * plain_part, axis=-1))
    along_cols = 4.0 * lax.optimization_barrier(jnp.sum(row_weight[None] * slope_part, axis=-1))
    grow_xx = 1.0 + time_step * along_rows[0]
    grow_xy = time_step * along_cols[0]
    grow_yx = time_step * along_rows[1]
    grow_yy = 1.0 + time_step * along_cols[1]
    upper_left, upper_right = (particles[8], particles[9])
    lower_left, lower_right = (particles[10], particles[11])
    return jnp.stack([position[0] + time_step * new_velocity[0], position[1] + time_step * new_velocity[1], new_velocity[0], new_velocity[1], along_rows[0], along_cols[0], along_rows[1], along_cols[1], grow_xx * upper_left + grow_xy * lower_left, grow_xx * upper_right + grow_xy * lower_right, grow_yx * upper_left + grow_yy * lower_left, grow_yx * upper_right + grow_yy * lower_right])

def place_rows(windows):
    padded_top = jnp.pad(windows[:, :, :BR], ((0, 1), (0, 0), (0, 0), (0, 0)))
    padded_low = jnp.pad(windows[:, :, BR:], ((1, 0), (0, 0), (0, 0), (0, 0)))
    slots_sum = padded_top + padded_low
    return jnp.moveaxis(slots_sum, 0, 1).reshape(slots_sum.shape[1], -1, slots_sum.shape[3])

def band_rows(extended):
    stacked = extended.reshape(extended.shape[0], -1, BR, extended.shape[2])
    paired = jnp.concatenate([stacked[:, :-1], stacked[:, 1:]], axis=2)
    return jnp.moveaxis(paired, 1, 0)

def scatter_pair(inputs):
    return scatter_band(inputs[0], inputs[1])

def gather_pair(inputs):
    return gather_band(inputs[0], inputs[1])

def gather_back(inputs):
    outputs, pullback = jax.vjp(gather_band, inputs[0], inputs[1])
    return pullback(inputs[2])

def scatter_back(inputs):
    outputs, pullback = jax.vjp(partial(scatter_band, alive_mask=inputs[1]), inputs[0])
    return pullback(inputs[2])[0]

def initial_particles(offsets, velocity, affine, strain):
    position = jnp.stack([BR // 2 + BR * offsets[0], BC // 2 + BC * offsets[1]])
    identity = jnp.array([1.0, 0.0, 0.0, 1.0], dtype=jnp.float32).reshape(4, 1, 1, 1)
    return jnp.concatenate([position, velocity, affine, strain + identity])

def fold_rows(extended):
    margin = BR // 2
    height = extended.shape[1] - BR
    interior = extended[:, margin:height + margin]
    low_rows = interior[:, :margin] + extended[:, height + margin:]
    high_rows = interior[:, height - margin:] + extended[:, :margin]
    return jnp.concatenate([low_rows, interior[:, margin:height - margin], high_rows], axis=1)

def wrap_rows(grid_field):
    margin = BR // 2
    return jnp.concatenate([grid_field[:, -margin:], grid_field, grid_field[:, :margin]], axis=1)

def reference(offsets, velocity, affine, strain, tile_fill, force_field, cotangent):
    alive_mask = (jnp.arange(P_SIZE, dtype=jnp.int32)[None, None, :] < tile_fill[:, :, None]).astype(jnp.float32)
    particles = initial_particles(offsets, velocity, affine, strain)
    history = []
    for step_index in range(STEPS):
        by_band = jnp.moveaxis(particles, 1, 0)
        summed = fold_rows(place_rows(lax.map(scatter_pair, (by_band, alive_mask))))
        inverse = 1.0 / (summed[0] + mass_floor)
        velocity_grid = (summed[1:3] + time_step * force_field) * inverse[None]
        history.append((particles, velocity_grid, inverse))
        particles = jnp.moveaxis(lax.map(gather_pair, (by_band, band_rows(wrap_rows(velocity_grid)))), 0, 1)
    adjoint = cotangent * alive_mask[None]
    force_grad = jnp.zeros_like(force_field)
    for step_index in reversed(range(STEPS)):
        particles, velocity_grid, inverse = history[step_index]
        by_band = jnp.moveaxis(particles, 1, 0)
        back_state, back_rows = lax.map(gather_back, (by_band, band_rows(wrap_rows(velocity_grid)), jnp.moveaxis(adjoint, 1, 0)))
        velocity_adjoint = fold_rows(place_rows(back_rows))
        momentum_adjoint = velocity_adjoint * inverse[None]
        mass_adjoint = -lax.optimization_barrier(jnp.sum(velocity_adjoint * velocity_grid, axis=0)) * inverse
        force_grad = force_grad + time_step * momentum_adjoint
        grid_adjoint = wrap_rows(jnp.concatenate([mass_adjoint[None], momentum_adjoint]))
        back_scatter = lax.map(scatter_back, (by_band, alive_mask, band_rows(grid_adjoint)))
        adjoint = jnp.moveaxis(back_state + back_scatter, 0, 1)
    scales = jnp.array([BR, BC], dtype=jnp.float32).reshape(2, 1, 1, 1)
    state_grad = jnp.concatenate([adjoint[0:2] * scales, adjoint[2:]])
    return (state_grad, force_grad)
```

```python
import functools

import jax
import jax.numpy as jnp
from jax import lax
from jax.experimental import pallas as pl
from jax.experimental.pallas import tpu as pltpu
from jax.sharding import PartitionSpec as P

STEPS = 4
DT = 0.1
MASS_FLOOR = 0.25
STRESS = -0.4
F32 = jnp.float32


def row_terms(p0, r, slopes=False):
    d = float(r) - p0
    m = jnp.abs(d)
    t = jnp.maximum(1.5 - m, 0.0)
    inner = m < 0.5
    w = jnp.where(inner, 0.75 - m * m, 0.5 * t * t)
    wd = w * d
    if not slopes:
        return w, wd
    dw = jnp.where(inner, 2.0 * d, jnp.where(d > 0.0, t, -t))
    return w, wd, dw, dw * d - w


def col_terms(p1, width, slopes=False):
    base = jnp.floor(jnp.clip(p1, -8.0, width + 8.0) - 0.5)
    bi = base.astype(jnp.int32)
    f = p1 - base
    d = [-f, 1.0 - f, 2.0 - f]
    up, down = 1.5 - f, f - 0.5
    w = [0.5 * up * up, 0.75 - d[1] * d[1], 0.5 * down * down]
    dw = [-up, 2.0 * d[1], down]
    idx, ws, wds, dws, dwds = [], [], [], [], []
    for k in range(3):
        node = bi + k
        valid = (node >= 0) & (node < width)
        idx.append(node & (width - 1))
        wk = jnp.where(valid, w[k], 0.0)
        ws.append(wk)
        wds.append(jnp.where(valid, wk * d[k], 0.0))
        if slopes:
            dk = jnp.where(valid, dw[k], 0.0)
            dws.append(dk)
            dwds.append(jnp.where(valid, dk * d[k] - wk, 0.0))
    if slopes:
        return idx, ws, wds, dws, dwds
    return idx, ws, wds


def comb(c, g):
    return c[0] * g[0] + c[1] * g[1] + c[2] * g[2]


def take(x, idx):
    return [jnp.take_along_axis(x, i, axis=1, mode="promise_in_bounds") for i in idx]


def kernel(n, br, bc, off, vel, aff, strn, fill, force, cot, sg, fg,
           hist, adj, alive, asc, wsc, ohs, nodes, vgrid, inv, fs, fsum,
           fsend, frecv, bsend, brecv, send_sem, recv_sem):
    nq = off.shape[1] // 2
    ps = off.shape[2]
    width = 2 * bc
    nr = 2 * br
    half = br // 2
    shape = (nq, ps)
    me = lax.axis_index("slab")
    right, left = lax.rem(me + 1, n), lax.rem(me + n - 1, n)
    mesh_id = pl.DeviceIdType.MESH
    barrier = pltpu.get_barrier_semaphore()
    for nb in (left, right):
        pl.semaphore_signal(barrier, inc=1, device_id=(nb,), device_id_type=mesh_id)

    lane = lax.broadcasted_iota(jnp.int32, shape, 1)
    sub = lax.broadcasted_iota(jnp.int32, shape, 0)

    def odd_window(g):
        rolled = pltpu.roll(g, bc, 1)
        return jnp.where(lane < bc, rolled, pltpu.roll(rolled, nq - 1, 0))

    def window(g, h):
        return g if h == 0 else odd_window(g)

    for h in range(2):
        own = pl.ds(h, nq, stride=2)
        lim = jnp.zeros(shape, jnp.int32)
        for q in range(nq):
            lim = jnp.where(sub == q, fill[0, 2 * q + h], lim)
        live = jnp.where(lane < lim, 1.0, 0.0).astype(F32)
        alive[h] = live
        hist[0, 0, h] = br // 2 + br * off[0, own, :]
        hist[0, 1, h] = bc // 2 + bc * off[1, own, :]
        for a in range(2):
            hist[0, 2 + a, h] = vel[a, own, :]
        for a in range(4):
            hist[0, 4 + a, h] = aff[a, own, :]
            hist[0, 8 + a, h] = strn[a, own, :] + (1.0 if a in (0, 3) else 0.0)
        for a in range(12):
            adj[a, h] = cot[a, own, :] * live

    shift = bc // 2
    for a in range(2):
        for q in range(nq):
            fs[pl.ds(a * br * nq + q, br, stride=nq), :] = force[a, :, q * ps:(q + 1) * ps]
    for a in range(2):
        for r in range(br):
            at = pl.ds((a * br + r) * nq, nq)
            rolled = pltpu.roll(fs[at, :], shift, 1)
            fs[at, :] = DT * jnp.where(lane >= shift, rolled, pltpu.roll(rolled, 1, 0))
            fsum[at, :] = jnp.zeros(shape, F32)

    pl.semaphore_wait(barrier, 2)

    def fill_columns(h, r, comp, plain, slope, ws, wds):
        for k in range(3):
            val = ws[k] * plain if slope is None else ws[k] * plain + wds[k] * slope
            asc[pl.ds(((h * 9 + comp * 3 + k) * nr + r) * nq, nq), :] = val

    def scatter(comps, step, fresh):
        rows = comps * 3 * nr
        iota_j = lax.broadcasted_iota(jnp.int32, (width, ps), 0)
        for q in range(nq):
            for h in range(2):
                part = asc[pl.ds(h * 9 * nr * nq + q, rows, stride=nq), :]
                hi = part.astype(jnp.bfloat16)
                lo = (part - hi.astype(F32)).astype(jnp.bfloat16)
                if fresh:
                    row = nodes[h, pl.ds(q, 1), :]
                    hot = jnp.where(iota_j == row, 1.0, 0.0).astype(jnp.bfloat16)
                    ohs[step, 2 * q + h] = hot
                else:
                    hot = ohs[step, 2 * q + h]
                res = lax.dot_general(
                    jnp.concatenate([hi, lo], axis=1), jnp.concatenate([hot, hot], axis=1),
                    (((1,), (1,)), ((), ())), preferred_element_type=F32)
                for comp in range(comps):
                    at = comp * 3 * nr
                    out = (res[at:at + nr] + pltpu.roll(res[at + nr:at + 2 * nr], 1, 1)
                           + pltpu.roll(res[at + 2 * nr:at + 3 * nr], 2, 1))
                    wsc[pl.ds((h * 3 + comp) * nr * nq + q, nr, stride=nq), :] = out

    def grid_row(comp, r):
        even = wsc[pl.ds((comp * nr + r) * nq, nq), :]
        odd = pltpu.roll(wsc[pl.ds(((3 + comp) * nr + r) * nq, nq), :], bc, 1)
        return even + jnp.where(lane >= bc, odd, pltpu.roll(odd, 1, 0))

    def exchange(send, recv, slot, sem):
        copies = []
        for side, to in ((0, left), (1, right)):
            copies.append(pltpu.make_async_remote_copy(
                src_ref=send.at[slot, side], dst_ref=recv.at[slot, side],
                send_sem=send_sem.at[sem, side], recv_sem=recv_sem.at[sem, side],
                device_id=(to,), device_id_type=mesh_id))
        for c in copies:
            c.start()
        return copies

    def summed(send, recv, slot, comp, r):
        side, rr = r // br, r % br
        return send[slot, side, comp, rr] + recv[slot, 1 - side, comp, rr]

    def stress_terms(st, h):
        f00, f01, f10, f11 = (hist[st, 8 + a, h] for a in range(4))
        jac = f00 * f11 - f01 * f10
        return f00, f01, f10, f11, jac

    def moments(st, h):
        live = alive[h]
        f00, f01, f10, f11, jac = stress_terms(st, h)
        pressure = 2.0 * (jac - 1.0) * jac
        s = live * STRESS
        xx = s * (2.0 * (f00 * f00 + f01 * f01 - 1.0) + pressure)
        xy = s * (2.0 * (f00 * f10 + f01 * f11))
        yy = s * (2.0 * (f10 * f10 + f11 * f11 - 1.0) + pressure)
        c = [hist[st, 4 + a, h] * live for a in range(4)]
        x = [live * hist[st, 2, h], live * hist[st, 3, h]]
        return live, x, [xx + c[0], xy + c[1], xy + c[2], yy + c[3]]

    def forward(st, carry):
        for h in range(2):
            live, x, m = moments(st, h)
            p0 = hist[st, 0, h]
            idx, ws, wds = col_terms(hist[st, 1, h], width)
            nodes[h] = idx[0]
            mws = [live * w for w in ws]
            for r in range(nr):
                w, wd = row_terms(p0, r)
                fill_columns(h, r, 0, w, None, mws, None)
                for a in range(2):
                    fill_columns(h, r, 1 + a, w * x[a] + wd * m[2 * a], w * m[2 * a + 1], ws, wds)
        scatter(3, st, True)
        for comp in range(3):
            for r in range(nr):
                g = grid_row(comp, r)
                if comp > 0 and half <= r < half + br:
                    g = g + fs[pl.ds(((comp - 1) * br + r - half) * nq, nq), :]
                fsend[st, r // br, comp, r % br] = g
        copies = exchange(fsend, frecv, st, st)
        for c in copies:
            c.wait()
        for r in range(nr):
            iv = 1.0 / (summed(fsend, frecv, st, 0, r) + MASS_FLOOR)
            inv[st, r] = iv
            for a in range(2):
                vgrid[st, a, r] = summed(fsend, frecv, st, 1 + a, r) * iv
        for h in range(2):
            p0, p1 = hist[st, 0, h], hist[st, 1, h]
            idx, ws, wds = col_terms(p1, width)
            v = [0.0, 0.0]
            along_rows = [0.0, 0.0]
            along_cols = [0.0, 0.0]
            for r in range(nr):
                w, wd = row_terms(p0, r)
                for a in range(2):
                    g = take(window(vgrid[st, a, r], h), idx)
                    plain, slope = comb(ws, g), comb(wds, g)
                    v[a] = v[a] + w * plain
                    along_rows[a] = along_rows[a] + wd * plain
                    along_cols[a] = along_cols[a] + w * slope
            c00, c10 = 4.0 * along_rows[0], 4.0 * along_rows[1]
            c01, c11 = 4.0 * along_cols[0], 4.0 * along_cols[1]
            f00, f01, f10, f11 = (hist[st, 8 + a, h] for a in range(4))
            gxx, gxy, gyx, gyy = 1.0 + DT * c00, DT * c01, DT * c10, 1.0 + DT * c11
            new = [p0 + DT * v[0], p1 + DT * v[1], v[0], v[1], c00, c01, c10, c11,
                   gxx * f00 + gxy * f10, gxx * f01 + gxy * f11,
                   gyx * f00 + gyy * f10, gyx * f01 + gyy * f11]
            for a in range(12):
                hist[st + 1, a, h] = new[a]
        return carry

    lax.fori_loop(0, STEPS, forward, 0)

    def backward(i, carry):
        st = STEPS - 1 - i
        for h in range(2):
            ab = [adj[a, h] for a in range(12)]
            f00, f01, f10, f11 = (hist[st, 8 + a, h] for a in range(4))
            x = [ab[2] + DT * ab[0], ab[3] + DT * ab[1]]
            m = [4.0 * (ab[4] + DT * (ab[8] * f00 + ab[9] * f01)),
                 4.0 * (ab[5] + DT * (ab[8] * f10 + ab[9] * f11)),
                 4.0 * (ab[6] + DT * (ab[10] * f00 + ab[11] * f01)),
                 4.0 * (ab[7] + DT * (ab[10] * f10 + ab[11] * f11))]
            p0 = hist[st, 0, h]
            idx, ws, wds = col_terms(hist[st, 1, h], width)
            for r in range(nr):
                w, wd = row_terms(p0, r)
                for a in range(2):
                    fill_columns(h, r, a, w * x[a] + wd * m[2 * a], w * m[2 * a + 1], ws, wds)
            adj[2, h], adj[3, h] = x[0], x[1]
            for a in range(4):
                adj[4 + a, h] = m[a]
        scatter(2, st, False)
        for comp in range(2):
            for r in range(nr):
                bsend[st, r // br, comp, r % br] = grid_row(comp, r)
        copies = exchange(bsend, brecv, st, STEPS + st)
        for h in range(2):
            p0 = hist[st, 0, h]
            idx, ws, wds, dws, dwds = col_terms(hist[st, 1, h], width, True)
            x = [adj[2 + a, h] for a in range(2)]
            m = [adj[4 + a, h] for a in range(4)]
            dp0, dp1 = adj[0, h], adj[1, h]
            for r in range(nr):
                w, wd, dw, dwd = row_terms(p0, r, True)
                u = t = du = dt = 0.0
                for a in range(2):
                    g = take(window(vgrid[st, a, r], h), idx)
                    plain, slope = comb(ws, g), comb(wds, g)
                    dplain, dslope = comb(dws, g), comb(dwds, g)
                    u = u + x[a] * plain + m[2 * a + 1] * slope
                    t = t + m[2 * a] * plain
                    du = du + x[a] * dplain + m[2 * a + 1] * dslope
                    dt = dt + m[2 * a] * dplain
                dp0 = dp0 + dw * u + dwd * t
                dp1 = dp1 + w * du + wd * dt
            adj[0, h], adj[1, h] = dp0, dp1
            c00, c01, c10, c11 = (hist[st + 1, 4 + a, h] for a in range(4))
            b00, b01, b10, b11 = (adj[8 + a, h] for a in range(4))
            gxx, gxy, gyx, gyy = 1.0 + DT * c00, DT * c01, DT * c10, 1.0 + DT * c11
            adj[8, h] = gxx * b00 + gyx * b10
            adj[9, h] = gxx * b01 + gyx * b11
            adj[10, h] = gxy * b00 + gyy * b10
            adj[11, h] = gxy * b01 + gyy * b11
        for c in copies:
            c.wait()
        for r in range(nr):
            iv = inv[st, r]
            v0, v1 = summed(bsend, brecv, st, 0, r), summed(bsend, brecv, st, 1, r)
            m0, m1 = v0 * iv, v1 * iv
            gm = -(v0 * vgrid[st, 0, r] + v1 * vgrid[st, 1, r]) * iv
            for comp, g in enumerate((gm, m0, m1)):
                wsc[pl.ds((comp * nr + r) * nq, nq), :] = g
            if half <= r < half + br:
                for a, g in enumerate((m0, m1)):
                    at = pl.ds((a * br + r - half) * nq, nq)
                    fsum[at, :] = fsum[at, :] + DT * g
        for h in range(2):
            live, x, m = moments(st, h)
            p0 = hist[st, 0, h]
            idx, ws, wds, dws, dwds = col_terms(hist[st, 1, h], width, True)
            dp0, dp1 = adj[0, h], adj[1, h]
            dx = [0.0, 0.0]
            dm = [0.0, 0.0, 0.0, 0.0]
            for r in range(nr):
                w, wd, dw, dwd = row_terms(p0, r, True)
                g = take(window(wsc[pl.ds(r * nq, nq), :], h), idx)
                u, du = live * comb(ws, g), live * comb(dws, g)
                t = dt = 0.0
                for a in range(2):
                    g = take(window(wsc[pl.ds(((1 + a) * nr + r) * nq, nq), :], h), idx)
                    plain, slope = comb(ws, g), comb(wds, g)
                    dplain, dslope = comb(dws, g), comb(dwds, g)
                    dx[a] = dx[a] + w * plain
                    dm[2 * a] = dm[2 * a] + wd * plain
                    dm[2 * a + 1] = dm[2 * a + 1] + w * slope
                    u = u + x[a] * plain + m[2 * a + 1] * slope
                    t = t + m[2 * a] * plain
                    du = du + x[a] * dplain + m[2 * a + 1] * dslope
                    dt = dt + m[2 * a] * dplain
                dp0 = dp0 + dw * u + dwd * t
                dp1 = dp1 + w * du + wd * dt
            adj[0, h], adj[1, h] = dp0, dp1
            for a in range(2):
                adj[2 + a, h] = live * dx[a]
            dm = [live * y for y in dm]
            for a in range(4):
                adj[4 + a, h] = dm[a]
            f00, f01, f10, f11, jac = stress_terms(st, h)
            txx, tyy, txy = STRESS * dm[0], STRESS * dm[3], STRESS * (dm[1] + dm[2])
            dj = (txx + tyy) * (2.0 * (2.0 * jac - 1.0))
            adj[8, h] = adj[8, h] + 4.0 * f00 * txx + 2.0 * f10 * txy + dj * f11
            adj[9, h] = adj[9, h] + 4.0 * f01 * txx + 2.0 * f11 * txy - dj * f10
            adj[10, h] = adj[10, h] + 4.0 * f10 * tyy + 2.0 * f00 * txy - dj * f01
            adj[11, h] = adj[11, h] + 4.0 * f11 * tyy + 2.0 * f01 * txy + dj * f00
        return carry

    lax.fori_loop(0, STEPS, backward, 0)

    for h in range(2):
        for a in range(12):
            scale = float(br) if a == 0 else float(bc)
            val = adj[a, h]
            sg[a, pl.ds(h, nq, stride=2), :] = scale * val if a < 2 else val
    for a in range(2):
        for r in range(br):
            at = pl.ds((a * br + r) * nq, nq)
            rolled = pltpu.roll(fsum[at, :], ps - shift, 1)
            fsum[at, :] = jnp.where(lane < ps - shift, rolled, pltpu.roll(rolled, nq - 1, 0))
    for a in range(2):
        for q in range(nq):
            fg[a, :, q * ps:(q + 1) * ps] = fsum[pl.ds(a * br * nq + q, br, stride=nq), :]


def solution(mesh):
    n = mesh.shape["slab"]

    def per_device(offsets, velocity, affine, strain, tile_fill, force_field, cotangent):
        blocks, ps = offsets.shape[2:]
        bands = offsets.shape[1]
        br = force_field.shape[1] // bands
        bc = force_field.shape[2] // blocks
        assert bands == 1 and ps == 2 * bc and blocks % 2 == 0
        nq, nr = blocks // 2, 2 * br
        flat = lambda x: x.reshape(x.shape[0], blocks, ps)
        vmem = pl.BlockSpec(memory_space=pltpu.VMEM)
        smem = pl.BlockSpec(memory_space=pltpu.SMEM)
        tile = (nq, ps)
        sg, fg = pl.pallas_call(
            functools.partial(kernel, n, br, bc),
            out_shape=(jax.ShapeDtypeStruct((12, blocks, ps), F32),
                       jax.ShapeDtypeStruct(force_field.shape, F32)),
            in_specs=[vmem, vmem, vmem, vmem, smem, vmem, vmem],
            out_specs=(vmem, vmem),
            scratch_shapes=[
                pltpu.VMEM((STEPS + 1, 12, 2) + tile, F32),
                pltpu.VMEM((12, 2) + tile, F32),
                pltpu.VMEM((2,) + tile, F32),
                pltpu.VMEM((2 * 9 * nr * nq, ps), F32),
                pltpu.VMEM((2 * 3 * nr * nq, ps), F32),
                pltpu.VMEM((STEPS, blocks, 2 * bc, ps), jnp.bfloat16),
                pltpu.VMEM((2,) + tile, jnp.int32),
                pltpu.VMEM((STEPS, 2, nr) + tile, F32),
                pltpu.VMEM((STEPS, nr) + tile, F32),
                pltpu.VMEM((2 * br * nq, ps), F32),
                pltpu.VMEM((2 * br * nq, ps), F32),
                pltpu.VMEM((STEPS, 2, 3, br) + tile, F32),
                pltpu.VMEM((STEPS, 2, 3, br) + tile, F32),
                pltpu.VMEM((STEPS, 2, 2, br) + tile, F32),
                pltpu.VMEM((STEPS, 2, 2, br) + tile, F32),
                pltpu.SemaphoreType.DMA((2 * STEPS, 2)),
                pltpu.SemaphoreType.DMA((2 * STEPS, 2)),
            ],
            compiler_params=pltpu.CompilerParams(collective_id=0, has_side_effects=True),
        )(flat(offsets), flat(velocity), flat(affine), flat(strain), tile_fill, force_field, flat(cotangent))
        return sg.reshape(12, 1, blocks, ps), fg

    cut = P(None, "slab", None, None)
    return jax.shard_map(
        per_device,
        mesh=mesh,
        in_specs=(cut, cut, cut, cut, P("slab", None), P(None, "slab", None), cut),
        out_specs=(cut, P(None, "slab", None)),
        check_vma=False,
    )
```

```python
import functools

import jax
import jax.numpy as jnp
from jax import lax
from jax.experimental import pallas as pl
from jax.experimental.pallas import tpu as pltpu
from jax.sharding import PartitionSpec as P

STEPS = 4
DT = 0.1
MASS_FLOOR = 0.25
STRESS = -0.4
F32 = jnp.float32


def row_terms(p0, r, slopes=False):
    d = r - p0
    m = jnp.abs(d)
    t = jnp.maximum(1.5 - m, 0.0)
    inner = m < 0.5
    w = jnp.where(inner, 0.75 - m * m, 0.5 * t * t)
    wd = w * d
    if not slopes:
        return w, wd
    dw = jnp.where(inner, 2.0 * d, jnp.where(d > 0.0, t, -t))
    return w, wd, dw, dw * d - w


def col_terms(p1, width, slopes=False):
    base = jnp.floor(jnp.clip(p1, -8.0, width + 8.0) - 0.5)
    bi = base.astype(jnp.int32)
    f = p1 - base
    d = [-f, 1.0 - f, 2.0 - f]
    up, down = 1.5 - f, f - 0.5
    w = [0.5 * up * up, 0.75 - d[1] * d[1], 0.5 * down * down]
    dw = [-up, 2.0 * d[1], down]
    idx, ws, wds, dws, dwds = [], [], [], [], []
    for k in range(3):
        node = bi + k
        valid = (node >= 0) & (node < width)
        idx.append(node & (width - 1))
        wk = jnp.where(valid, w[k], 0.0)
        ws.append(wk)
        wds.append(jnp.where(valid, wk * d[k], 0.0))
        if slopes:
            dk = jnp.where(valid, dw[k], 0.0)
            dws.append(dk)
            dwds.append(jnp.where(valid, dk * d[k] - wk, 0.0))
    if slopes:
        return idx, ws, wds, dws, dwds
    return idx, ws, wds


def comb(c, g):
    return c[0] * g[0] + c[1] * g[1] + c[2] * g[2]


def take(x, idx):
    return [jnp.take_along_axis(x, i, axis=1, mode="promise_in_bounds") for i in idx]


def kernel(n, br, bc, off, vel, aff, strn, fill, force, cot, sg, fg,
           hist, adj, alive, asc, wsc, ohs, nodes, vgrid, inv, fs, fext, fsum,
           fsend, frecv, bsend, brecv, send_sem, recv_sem):
    nq = off.shape[1] // 2
    ps = off.shape[2]
    width = 2 * bc
    nr = 2 * br
    half = br // 2
    shape = (nq, ps)
    me = lax.axis_index("slab")
    right, left = lax.rem(me + 1, n), lax.rem(me + n - 1, n)
    first = lax.rem(me // 2, 2)
    near = 1 - lax.rem(me, 2)
    mesh_id = pl.DeviceIdType.MESH
    barrier = pltpu.get_barrier_semaphore()
    for nb in (left, right):
        pl.semaphore_signal(barrier, inc=1, device_id=(nb,), device_id_type=mesh_id)

    lane = lax.broadcasted_iota(jnp.int32, shape, 1)
    sub = lax.broadcasted_iota(jnp.int32, shape, 0)

    def odd_window(g):
        rolled = pltpu.roll(g, bc, 1)
        return jnp.where(lane < bc, rolled, pltpu.roll(rolled, nq - 1, 0))

    def window(g, h):
        return g if h == 0 else odd_window(g)

    for h in range(2):
        own = pl.ds(h, nq, stride=2)
        lim = jnp.zeros(shape, jnp.int32)
        for q in range(nq):
            lim = jnp.where(sub == q, fill[0, 2 * q + h], lim)
        live = jnp.where(lane < lim, 1.0, 0.0).astype(F32)
        alive[h] = live
        hist[0, 0, h] = br // 2 + br * off[0, own, :]
        hist[0, 1, h] = bc // 2 + bc * off[1, own, :]
        for a in range(2):
            hist[0, 2 + a, h] = vel[a, own, :]
        for a in range(4):
            hist[0, 4 + a, h] = aff[a, own, :]
            hist[0, 8 + a, h] = strn[a, own, :] + (1.0 if a in (0, 3) else 0.0)
        for a in range(12):
            adj[a, h] = cot[a, own, :] * live

    shift = bc // 2
    for a in range(2):
        for q in range(nq):
            fs[pl.ds(a * br * nq + q, br, stride=nq), :] = force[a, :, q * ps:(q + 1) * ps]
    for a in range(2):
        for r in range(nr):
            fsum[a, r] = jnp.zeros(shape, F32)
            fext[a, r] = jnp.zeros(shape, F32)
        for r in range(br):
            rolled = pltpu.roll(fs[pl.ds((a * br + r) * nq, nq), :], shift, 1)
            fext[a, r + half] = DT * jnp.where(lane >= shift, rolled, pltpu.roll(rolled, 1, 0))
    asc[...] = jnp.zeros_like(asc)

    pl.semaphore_wait(barrier, 2)

    def padded(comps):
        return -(-comps * br // 8) * 8

    def fill_columns(phase, comps, h, rr, comp, plain, slope, ws, wds):
        kb = padded(comps)
        for k in range(3):
            val = ws[k] * plain if slope is None else ws[k] * plain + wds[k] * slope
            at = ((phase * 2 + h) * 3 * padded(3) + k * kb + comp * br + rr) * nq
            asc[pl.ds(at, nq), :] = val

    def scatter(phase, comps, step, fresh):
        kb = padded(comps)
        iota_j = lax.broadcasted_iota(jnp.int32, (width, ps), 0)
        for q in range(nq):
            for h in range(2):
                part = asc[pl.ds((phase * 2 + h) * 3 * padded(3) * nq + q, 3 * kb, stride=nq), :]
                hi = part.astype(jnp.bfloat16)
                lo = (part - hi.astype(F32)).astype(jnp.bfloat16)
                if fresh:
                    row = nodes[h, pl.ds(q, 1), :]
                    hot = jnp.where(iota_j == row, 1.0, 0.0).astype(jnp.bfloat16)
                    ohs[step, 2 * q + h] = hot
                else:
                    hot = ohs[step, 2 * q + h]
                res = lax.dot_general(
                    jnp.concatenate([hi, lo], axis=1), jnp.concatenate([hot, hot], axis=1),
                    (((1,), (1,)), ((), ())), preferred_element_type=F32)
                out = res[:kb] + pltpu.roll(res[kb:2 * kb], 1, 1) + pltpu.roll(res[2 * kb:], 2, 1)
                wsc[pl.ds((phase * 2 + h) * padded(3) * nq + q, kb, stride=nq), :] = out

    def grid_row(phase, comp, rr):
        even = wsc[pl.ds((phase * 2 * padded(3) + comp * br + rr) * nq, nq), :]
        odd = pltpu.roll(wsc[pl.ds(((phase * 2 + 1) * padded(3) + comp * br + rr) * nq, nq), :], bc, 1)
        return even + jnp.where(lane >= bc, odd, pltpu.roll(odd, 1, 0))

    def copy_of(send, recv, slot, sem, side):
        return pltpu.make_async_remote_copy(
            src_ref=send.at[slot, side], dst_ref=recv.at[slot, side],
            send_sem=send_sem.at[sem, side], recv_sem=recv_sem.at[sem, side],
            device_id=(lax.rem(me + n - 1 + 2 * side, n),), device_id_type=mesh_id)

    def summed(send, recv, slot, side, comp, rr):
        return send[slot, side, comp, rr] + recv[slot, 1 - side, comp, rr]

    def stress_terms(st, h):
        f00, f01, f10, f11 = (hist[st, 8 + a, h] for a in range(4))
        jac = f00 * f11 - f01 * f10
        return f00, f01, f10, f11, jac

    def moments(st, h):
        live = alive[h]
        f00, f01, f10, f11, jac = stress_terms(st, h)
        pressure = 2.0 * (jac - 1.0) * jac
        s = live * STRESS
        xx = s * (2.0 * (f00 * f00 + f01 * f01 - 1.0) + pressure)
        xy = s * (2.0 * (f00 * f10 + f01 * f11))
        yy = s * (2.0 * (f10 * f10 + f11 * f11 - 1.0) + pressure)
        c = [hist[st, 4 + a, h] * live for a in range(4)]
        x = [live * hist[st, 2, h], live * hist[st, 3, h]]
        return live, x, [xx + c[0], xy + c[1], xy + c[2], yy + c[3]]

    def forward(st, carry):
        cols = []
        for h in range(2):
            cols.append(col_terms(hist[st, 1, h], width))
            nodes[h] = cols[h][0][0]
        for phase in range(2):
            side = first if phase == 0 else 1 - first
            for h in range(2):
                live, x, m = moments(st, h)
                p0 = hist[st, 0, h]
                idx, ws, wds = cols[h]
                mws = [live * w for w in ws]
                for rr in range(br):
                    w, wd = row_terms(p0, (side * br + rr).astype(F32))
                    fill_columns(phase, 3, h, rr, 0, w, None, mws, None)
                    for a in range(2):
                        fill_columns(phase, 3, h, rr, 1 + a, w * x[a] + wd * m[2 * a], w * m[2 * a + 1], ws, wds)
            scatter(phase, 3, st, phase == 0)
            for comp in range(3):
                for rr in range(br):
                    g = grid_row(phase, comp, rr)
                    if comp > 0:
                        g = g + fext[comp - 1, side * br + rr]
                    fsend[st, side, comp, rr] = g
            copy_of(fsend, frecv, st, st, side).start()
        acc = [[0.0] * 6 for h in range(2)]
        for part in range(2):
            side = near if part == 0 else 1 - near
            copy_of(fsend, frecv, st, st, 1 - side).wait_recv()
            for rr in range(br):
                r = side * br + rr
                iv = 1.0 / (summed(fsend, frecv, st, side, 0, rr) + MASS_FLOOR)
                inv[st, r] = iv
                vg = [summed(fsend, frecv, st, side, 1 + a, rr) * iv for a in range(2)]
                for a in range(2):
                    vgrid[st, a, r] = vg[a]
                for h in range(2):
                    idx, ws, wds = cols[h]
                    w, wd = row_terms(hist[st, 0, h], r.astype(F32))
                    for a in range(2):
                        g = take(window(vg[a], h), idx)
                        plain, slope = comb(ws, g), comb(wds, g)
                        acc[h][a] = acc[h][a] + w * plain
                        acc[h][2 + a] = acc[h][2 + a] + wd * plain
                        acc[h][4 + a] = acc[h][4 + a] + w * slope
        for side in range(2):
            copy_of(fsend, frecv, st, st, side).wait_send()
        for h in range(2):
            p0, p1 = hist[st, 0, h], hist[st, 1, h]
            v, along_rows, along_cols = acc[h][0:2], acc[h][2:4], acc[h][4:6]
            c00, c10 = 4.0 * along_rows[0], 4.0 * along_rows[1]
            c01, c11 = 4.0 * along_cols[0], 4.0 * along_cols[1]
            f00, f01, f10, f11 = (hist[st, 8 + a, h] for a in range(4))
            gxx, gxy, gyx, gyy = 1.0 + DT * c00, DT * c01, DT * c10, 1.0 + DT * c11
            new = [p0 + DT * v[0], p1 + DT * v[1], v[0], v[1], c00, c01, c10, c11,
                   gxx * f00 + gxy * f10, gxx * f01 + gxy * f11,
                   gyx * f00 + gyy * f10, gyx * f01 + gyy * f11]
            for a in range(12):
                hist[st + 1, a, h] = new[a]
        return carry

    lax.fori_loop(0, STEPS, forward, 0)

    def backward(i, carry):
        st = STEPS - 1 - i
        for h in range(2):
            ab = [adj[a, h] for a in range(12)]
            f00, f01, f10, f11 = (hist[st, 8 + a, h] for a in range(4))
            x = [ab[2] + DT * ab[0], ab[3] + DT * ab[1]]
            m = [4.0 * (ab[4] + DT * (ab[8] * f00 + ab[9] * f01)),
                 4.0 * (ab[5] + DT * (ab[8] * f10 + ab[9] * f11)),
                 4.0 * (ab[6] + DT * (ab[10] * f00 + ab[11] * f01)),
                 4.0 * (ab[7] + DT * (ab[10] * f10 + ab[11] * f11))]
            adj[2, h], adj[3, h] = x[0], x[1]
            for a in range(4):
                adj[4 + a, h] = m[a]
        for phase in range(2):
            side = first if phase == 0 else 1 - first
            for h in range(2):
                x = [adj[2 + a, h] for a in range(2)]
                m = [adj[4 + a, h] for a in range(4)]
                p0 = hist[st, 0, h]
                idx, ws, wds = col_terms(hist[st, 1, h], width)
                for rr in range(br):
                    w, wd = row_terms(p0, (side * br + rr).astype(F32))
                    for a in range(2):
                        fill_columns(phase, 2, h, rr, a, w * x[a] + wd * m[2 * a], w * m[2 * a + 1], ws, wds)
            scatter(phase, 2, st, False)
            for comp in range(2):
                for rr in range(br):
                    bsend[st, side, comp, rr] = grid_row(phase, comp, rr)
            copy_of(bsend, brecv, st, STEPS + st, side).start()
        for h in range(2):
            p0 = hist[st, 0, h]
            idx, ws, wds, dws, dwds = col_terms(hist[st, 1, h], width, True)
            x = [adj[2 + a, h] for a in range(2)]
            m = [adj[4 + a, h] for a in range(4)]
            dp0, dp1 = adj[0, h], adj[1, h]
            for r in range(nr):
                w, wd, dw, dwd = row_terms(p0, float(r), True)
                u = t = du = dt = 0.0
                for a in range(2):
                    g = take(window(vgrid[st, a, r], h), idx)
                    plain, slope = comb(ws, g), comb(wds, g)
                    dplain, dslope = comb(dws, g), comb(dwds, g)
                    u = u + x[a] * plain + m[2 * a + 1] * slope
                    t = t + m[2 * a] * plain
                    du = du + x[a] * dplain + m[2 * a + 1] * dslope
                    dt = dt + m[2 * a] * dplain
                dp0 = dp0 + dw * u + dwd * t
                dp1 = dp1 + w * du + wd * dt
            adj[0, h], adj[1, h] = dp0, dp1
            c00, c01, c10, c11 = (hist[st + 1, 4 + a, h] for a in range(4))
            b00, b01, b10, b11 = (adj[8 + a, h] for a in range(4))
            gxx, gxy, gyx, gyy = 1.0 + DT * c00, DT * c01, DT * c10, 1.0 + DT * c11
            adj[8, h] = gxx * b00 + gyx * b10
            adj[9, h] = gxx * b01 + gyx * b11
            adj[10, h] = gxy * b00 + gyy * b10
            adj[11, h] = gxy * b01 + gyy * b11
        parts = []
        for h in range(2):
            parts.append([moments(st, h), col_terms(hist[st, 1, h], width, True), [0.0] * 6,
                          [adj[0, h], adj[1, h]]])
        for part in range(2):
            side = near if part == 0 else 1 - near
            copy_of(bsend, brecv, st, STEPS + st, 1 - side).wait_recv()
            for rr in range(br):
                r = side * br + rr
                iv = inv[st, r]
                v0, v1 = (summed(bsend, brecv, st, side, a, rr) for a in range(2))
                gs = [v0 * iv, v1 * iv]
                gm = -(v0 * vgrid[st, 0, r] + v1 * vgrid[st, 1, r]) * iv
                for a in range(2):
                    fsum[a, r] = fsum[a, r] + DT * gs[a]
                for h in range(2):
                    (live, x, m), (idx, ws, wds, dws, dwds), acc, dp = parts[h]
                    w, wd, dw, dwd = row_terms(hist[st, 0, h], r.astype(F32), True)
                    g = take(window(gm, h), idx)
                    u, du = live * comb(ws, g), live * comb(dws, g)
                    t = dt = 0.0
                    for a in range(2):
                        g = take(window(gs[a], h), idx)
                        plain, slope = comb(ws, g), comb(wds, g)
                        dplain, dslope = comb(dws, g), comb(dwds, g)
                        acc[a] = acc[a] + w * plain
                        acc[2 + 2 * a] = acc[2 + 2 * a] + wd * plain
                        acc[3 + 2 * a] = acc[3 + 2 * a] + w * slope
                        u = u + x[a] * plain + m[2 * a + 1] * slope
                        t = t + m[2 * a] * plain
                        du = du + x[a] * dplain + m[2 * a + 1] * dslope
                        dt = dt + m[2 * a] * dplain
                    dp[0] = dp[0] + dw * u + dwd * t
                    dp[1] = dp[1] + w * du + wd * dt
        for side in range(2):
            copy_of(bsend, brecv, st, STEPS + st, side).wait_send()
        for h in range(2):
            (live, x, m), _, acc, (dp0, dp1) = parts[h]
            dx, dm = acc[:2], acc[2:]
            adj[0, h], adj[1, h] = dp0, dp1
            for a in range(2):
                adj[2 + a, h] = live * dx[a]
            dm = [live * y for y in dm]
            for a in range(4):
                adj[4 + a, h] = dm[a]
            f00, f01, f10, f11, jac = stress_terms(st, h)
            txx, tyy, txy = STRESS * dm[0], STRESS * dm[3], STRESS * (dm[1] + dm[2])
            dj = (txx + tyy) * (2.0 * (2.0 * jac - 1.0))
            adj[8, h] = adj[8, h] + 4.0 * f00 * txx + 2.0 * f10 * txy + dj * f11
            adj[9, h] = adj[9, h] + 4.0 * f01 * txx + 2.0 * f11 * txy - dj * f10
            adj[10, h] = adj[10, h] + 4.0 * f10 * tyy + 2.0 * f00 * txy - dj * f01
            adj[11, h] = adj[11, h] + 4.0 * f11 * tyy + 2.0 * f01 * txy + dj * f00
        return carry

    lax.fori_loop(0, STEPS, backward, 0)

    for h in range(2):
        for a in range(12):
            scale = float(br) if a == 0 else float(bc)
            val = adj[a, h]
            sg[a, pl.ds(h, nq, stride=2), :] = scale * val if a < 2 else val
    for a in range(2):
        for r in range(br):
            rolled = pltpu.roll(fsum[a, half + r], ps - shift, 1)
            fs[pl.ds((a * br + r) * nq, nq), :] = jnp.where(
                lane < ps - shift, rolled, pltpu.roll(rolled, nq - 1, 0))
    for a in range(2):
        for q in range(nq):
            fg[a, :, q * ps:(q + 1) * ps] = fs[pl.ds(a * br * nq + q, br, stride=nq), :]


def solution(mesh):
    n = mesh.shape["slab"]

    def per_device(offsets, velocity, affine, strain, tile_fill, force_field, cotangent):
        blocks, ps = offsets.shape[2:]
        bands = offsets.shape[1]
        br = force_field.shape[1] // bands
        bc = force_field.shape[2] // blocks
        assert bands == 1 and ps == 2 * bc and blocks % 2 == 0
        nq, nr = blocks // 2, 2 * br
        pad = -(-3 * br // 8) * 8
        flat = lambda x: x.reshape(x.shape[0], blocks, ps)
        vmem = pl.BlockSpec(memory_space=pltpu.VMEM)
        smem = pl.BlockSpec(memory_space=pltpu.SMEM)
        tile = (nq, ps)
        sg, fg = pl.pallas_call(
            functools.partial(kernel, n, br, bc),
            out_shape=(jax.ShapeDtypeStruct((12, blocks, ps), F32),
                       jax.ShapeDtypeStruct(force_field.shape, F32)),
            in_specs=[vmem, vmem, vmem, vmem, smem, vmem, vmem],
            out_specs=(vmem, vmem),
            scratch_shapes=[
                pltpu.VMEM((STEPS + 1, 12, 2) + tile, F32),
                pltpu.VMEM((12, 2) + tile, F32),
                pltpu.VMEM((2,) + tile, F32),
                pltpu.VMEM((4 * 3 * pad * nq, ps), F32),
                pltpu.VMEM((4 * pad * nq, ps), F32),
                pltpu.VMEM((STEPS, blocks, 2 * bc, ps), jnp.bfloat16),
                pltpu.VMEM((2,) + tile, jnp.int32),
                pltpu.VMEM((STEPS, 2, nr) + tile, F32),
                pltpu.VMEM((STEPS, nr) + tile, F32),
                pltpu.VMEM((2 * br * nq, ps), F32),
                pltpu.VMEM((2, nr) + tile, F32),
                pltpu.VMEM((2, nr) + tile, F32),
                pltpu.VMEM((STEPS, 2, 3, br) + tile, F32),
                pltpu.VMEM((STEPS, 2, 3, br) + tile, F32),
                pltpu.VMEM((STEPS, 2, 2, br) + tile, F32),
                pltpu.VMEM((STEPS, 2, 2, br) + tile, F32),
                pltpu.SemaphoreType.DMA((2 * STEPS, 2)),
                pltpu.SemaphoreType.DMA((2 * STEPS, 2)),
            ],
            compiler_params=pltpu.CompilerParams(collective_id=0, has_side_effects=True),
        )(flat(offsets), flat(velocity), flat(affine), flat(strain), tile_fill, force_field, flat(cotangent))
        return sg.reshape(12, 1, blocks, ps), fg

    cut = P(None, "slab", None, None)
    return jax.shard_map(
        per_device,
        mesh=mesh,
        in_specs=(cut, cut, cut, cut, P("slab", None), P(None, "slab", None), cut),
        out_specs=(cut, P(None, "slab", None)),
        check_vma=False,
    )
```
